32 devices in a mesh: dp: 32 (over z, y, x, core).
Axes of the slice: x: 2, y: 2, z: 4, core: 2. Of those that a mesh axis runs over, the one named last changes fastest.
Arguments:
- block_input: bfloat16 [4096, 1088], P('dp'), may hold values from -6 to 6
- out_cotangent: bfloat16 [4096, 1088], P('dp'), may hold values from -6 to 6
- seq_lengths: int32 [32, 4], P('dp'), may hold values from 1 to 64, 128 in all within a row
- w_qkv: bfloat16 [3551232], P('dp'), may hold values from -1 to 1
- w_out: bfloat16 [1183744], P('dp'), may hold values from -0.75 to 0.75
- w_up: bfloat16 [4734976], P('dp'), may hold values from -0.1875 to 0.1875
- w_down: bfloat16 [4734976], P('dp'), may hold values from -0.09375 to 0.09375
- vectors: bfloat16 [13056], P('dp'), may hold values from 0.099609375 to 1.8984375
Outputs:
- block_output: bfloat16 [4096, 1088], P('dp')
- input_grad: float32 [4096, 1088], P('dp')
- grad_qkv: float32 [3551232], P('dp')
- grad_out: float32 [1183744], P('dp')
- grad_up: float32 [4734976], P('dp')
- grad_down: float32 [4734976], P('dp')
- grad_vectors: float32 [13056], P('dp')
The draws below stay inside these ranges and needn't reach their ends.
Inputs may be any that keep to these rules, and one draw needn't show every extreme that they name: `seq_lengths`: in every row the lengths sum to 128; the longest sequence has 64 tokens.
All inputs are finite; a program needn't handle non-finite values.
Results may differ from the reference program's by a relative error of at most 0.012.
The reference program's roundings to bfloat16 on the way count: a program that leaves them out, or rounds other values in their place, can miss the bound.
Values may be sent and summed in bfloat16 or wider, within the bound.
A program may use at most 320 MiB of HBM per device.

```python
import math
import jax
import jax.numpy as jnp
import numpy as np
from jax import lax

HEADS = 17
HEAD_DIM = 64
D = 1088
FF = 4352
TOK_DEV = 128
SEQS = 4
MOST = 64
TOKENS = 4096
N_DP = 32


def draw_block_input(key, part):
    own = jax.random.fold_in(key, 31)
    values = jax.random.truncated_normal(own, -6.0, 6.0, (TOKENS, D), jnp.float32)
    return values.astype(jnp.bfloat16)


def draw_w_qkv(key, part):
    own = jax.random.fold_in(key, 47)
    spread = D ** (-0.5)
    base = jax.random.truncated_normal(own, -6.0, 6.0, (D, 3 * D), jnp.float32) * spread
    return base.reshape(3 * D * D).astype(jnp.bfloat16)


def steps_of(rng, dims, pieces, smallest, top_value):
    loudness, own = 1.0, jax.random.fold_in(rng, 6)
    for axis_at, parts in pieces:
        heights = jnp.exp(jax.random.uniform(jax.random.fold_in(own, axis_at), (parts,), jnp.float32, smallest / len(pieces), top_value / len(pieces)))
        loudness = loudness * jnp.repeat(heights, dims[axis_at] // parts).reshape([-1 if axis == axis_at else 1 for axis in range(len(dims))])
    return loudness


def split_up(amount, total, limit, lean):
    weights = [(1 << 20) // math.isqrt(grade ** lean) + 1 for grade in range(2, amount + 1)]
    spare, counts = total - limit - (amount - 1), [1] * (amount - 1)
    while spare > 0:
        free = [i for i in range(amount - 1) if counts[i] < limit]
        whole, remaining = sum([weights[i] for i in free]), spare
        for i in free:
            more = min(limit - counts[i], max(1, remaining * weights[i] // whole), spare)
            counts[i] = counts[i] + more
            spare = spare - more
    return np.array([limit] + counts)


def uneven_parts(own_key, number_of, total, most, slope):
    if number_of == 2:
        one = jax.random.randint(own_key, (), max(1, total - most), min(most, total - 1) + 1)
        return jnp.stack([one, total - one])
    tallies = jnp.asarray(split_up(number_of, total, most, slope), jnp.int32)
    couples = (number_of - 1) // 2
    donor, taker = tallies[1:1 + 2 * couples:2], tallies[2:2 + 2 * couples:2]
    slack = jnp.minimum(donor - 1, most - taker)
    shifted = jax.random.randint(jax.random.fold_in(own_key, 1), (couples,), 0, 1 << 20) % (slack + 1)
    tallies = tallies.at[1:1 + 2 * couples:2].set(donor - shifted).at[2:2 + 2 * couples:2].set(taker + shifted)
    return tallies[jax.random.permutation(jax.random.fold_in(own_key, 2), number_of)]


def scatter_about(stream_key, dims, scale, most, shards=(), kind=jnp.bfloat16):
    array = scale * jax.random.normal(stream_key, dims, jnp.float32)
    if shards:
        array = array * steps_of(stream_key, dims, shards, -0.22, 0.18)
    return jnp.clip(array, -most, most).astype(kind)


def setup_inputs(seed: int = 0) -> dict:
    streams_of = jax.random.split(jax.random.key(seed), 9)
    block_input = draw_block_input(jax.random.fold_in(streams_of[8], 71), 0)
    out_cotangent = scatter_about(streams_of[1], (TOKENS, D), 1.0, 6.0, ((0, 32),))
    seq_lengths = jax.vmap(lambda own: uneven_parts(own, SEQS, TOK_DEV, MOST, 2))(jax.random.split(streams_of[2], N_DP)).reshape((N_DP, SEQS)).astype(jnp.int32)
    w_qkv = draw_w_qkv(jax.random.fold_in(streams_of[8], 71), 0)
    w_out = scatter_about(streams_of[4], (D * D,), (D // 16) ** -0.5, 0.75, ((0, 32),))
    w_up = scatter_about(streams_of[5], (D * FF,), D ** -0.5, 0.1875, ((0, 32),))
    w_down = scatter_about(streams_of[6], (FF * D,), FF ** -0.5, 0.09375, ((0, 32),))
    vectors = jnp.clip(1.0 + 0.18 * jax.random.normal(streams_of[7], (8 * D + FF,), jnp.float32), 0.099609375, 1.8984375).astype(jnp.bfloat16)
    return {"block_input": block_input, "out_cotangent": out_cotangent, "seq_lengths": seq_lengths, "w_qkv": w_qkv, "w_out": w_out, "w_up": w_up, "w_down": w_down, "vectors": vectors}


EPS = 1e-05
ROOT_HALF = 0.7071067811865476
INV_ROOT_TAU = 0.3989422804014327

def layer_norm(rows, gain, shift):
    mean = lax.optimization_barrier(jnp.mean(rows, axis=1, keepdims=True))
    centered = rows - mean
    inverse = lax.rsqrt(lax.optimization_barrier(jnp.mean(centered * centered, axis=1, keepdims=True)) + EPS)
    normed = centered * inverse
    return (normed, inverse, normed * gain + shift)

def norm_back(grad_rows, normed, inverse, gain):
    scaled = grad_rows * gain
    inner = lax.optimization_barrier(jnp.mean(scaled * normed, axis=1, keepdims=True))
    return inverse * (scaled - lax.optimization_barrier(jnp.mean(scaled, axis=1, keepdims=True)) - normed * inner)

def gelu_exact(value):
    return 0.5 * value * (1.0 + lax.erf(value * ROOT_HALF))

def gelu_slope(value):
    return 0.5 * (1.0 + lax.erf(value * ROOT_HALF)) + value * jnp.exp(-0.5 * value * value) * INV_ROOT_TAU

def causal_mask(lengths, rows):
    ends = jnp.cumsum(lengths.astype(jnp.int32))
    position = jnp.arange(rows, dtype=jnp.int32)
    segment = lax.optimization_barrier(jnp.sum((position[:, None] >= ends[None, :]).astype(jnp.int32), axis=1))
    return (segment[:, None] == segment[None, :]) & (position[None, :] <= position[:, None])

def score_block(query, keys, mask):
    scores = jnp.einsum('qhe,khe->hqk', query.astype(jnp.float32), keys.astype(jnp.float32))
    return jnp.where(mask[None], scores, -1e+30)

def device_pass(block, cotangent, lengths, wqkv, wo, wup, wdn, vec):
    rows = block.shape[0]
    scale = HEAD_DIM ** (-0.5)
    mask = causal_mask(lengths, rows)
    inputs = block.astype(jnp.float32)
    normed1, inverse1, pre1 = layer_norm(inputs, vec[0:D], vec[D:2 * D])
    first = pre1.astype(jnp.bfloat16)
    qkv = jnp.dot(first, wqkv, preferred_element_type=jnp.float32)
    query = ((qkv[:, 0:D] + vec[2 * D:3 * D]) * scale).astype(jnp.bfloat16).reshape(rows, HEADS, HEAD_DIM)
    keys = qkv[:, D:2 * D].astype(jnp.bfloat16).reshape(rows, HEADS, HEAD_DIM)
    values = (qkv[:, 2 * D:3 * D] + vec[3 * D:4 * D]).astype(jnp.bfloat16).reshape(rows, HEADS, HEAD_DIM)
    scores = score_block(query, keys, mask)
    peak = lax.optimization_barrier(jnp.max(scores, axis=2, keepdims=True))
    logsum = peak + jnp.log(lax.optimization_barrier(jnp.sum(jnp.exp(scores - peak), axis=2, keepdims=True)))
    probs_low = jnp.exp(scores - logsum).astype(jnp.bfloat16)
    mixed = jnp.einsum('hqk,khe->qhe', probs_low.astype(jnp.float32), values.astype(jnp.float32))
    mixed = mixed.astype(jnp.bfloat16).reshape(rows, D)
    resid = inputs + jnp.dot(mixed, wo, preferred_element_type=jnp.float32) + vec[4 * D:5 * D]
    normed2, inverse2, pre2 = layer_norm(resid, vec[5 * D:6 * D], vec[6 * D:7 * D])
    second = pre2.astype(jnp.bfloat16)
    upper = jnp.dot(second, wup, preferred_element_type=jnp.float32) + vec[7 * D:7 * D + FF]
    active = gelu_exact(upper).astype(jnp.bfloat16)
    output = (resid + jnp.dot(active, wdn, preferred_element_type=jnp.float32) + vec[7 * D + FF:]).astype(jnp.bfloat16)
    grad_top = cotangent.astype(jnp.float32)
    grad_low = cotangent
    g_down = jnp.dot(active.T, grad_low, preferred_element_type=jnp.float32)
    d_upper = jnp.dot(grad_low, wdn.T, preferred_element_type=jnp.float32) * gelu_slope(upper)
    d_upper_low = d_upper.astype(jnp.bfloat16)
    g_up = jnp.dot(second.T, d_upper_low, preferred_element_type=jnp.float32)
    d_second = jnp.dot(d_upper_low, wup.T, preferred_element_type=jnp.float32)
    d_resid = grad_top + norm_back(d_second, normed2, inverse2, vec[5 * D:6 * D])
    d_resid_low = d_resid.astype(jnp.bfloat16)
    g_out = jnp.dot(mixed.T, d_resid_low, preferred_element_type=jnp.float32)
    d_mixed = jnp.dot(d_resid_low, wo.T, preferred_element_type=jnp.float32).astype(jnp.bfloat16)
    d_mixed = d_mixed.reshape(rows, HEADS, HEAD_DIM)
    probs = jnp.exp(score_block(query, keys, mask) - logsum)
    probs_low = probs.astype(jnp.bfloat16)
    d_values = jnp.einsum('hqk,qhe->khe', probs_low.astype(jnp.float32), d_mixed.astype(jnp.float32))
    d_probs = jnp.einsum('qhe,khe->hqk', d_mixed.astype(jnp.float32), values.astype(jnp.float32))
    delta = lax.optimization_barrier(jnp.sum(probs * d_probs, axis=2, keepdims=True))
    d_scores = (probs * (d_probs - delta)).astype(jnp.bfloat16).astype(jnp.float32)
    d_query = jnp.einsum('hqk,khe->qhe', d_scores, keys.astype(jnp.float32)).reshape(rows, D) * scale
    d_keys = jnp.einsum('hqk,qhe->khe', d_scores, query.astype(jnp.float32)).reshape(rows, D)
    d_values = d_values.reshape(rows, D)
    d_qkv = jnp.concatenate([d_query, d_keys, d_values], axis=1).astype(jnp.bfloat16)
    g_qkv = jnp.dot(first.T, d_qkv, preferred_element_type=jnp.float32)
    d_first = jnp.dot(d_qkv, wqkv.T, preferred_element_type=jnp.float32)
    d_input = d_resid + norm_back(d_first, normed1, inverse1, vec[0:D])
    g_vec = jnp.concatenate([lax.optimization_barrier(jnp.sum(d_first * normed1, axis=0)), lax.optimization_barrier(jnp.sum(d_first, axis=0)), lax.optimization_barrier(jnp.sum(d_query, axis=0)), lax.optimization_barrier(jnp.sum(d_values, axis=0)), lax.optimization_barrier(jnp.sum(d_resid, axis=0)), lax.optimization_barrier(jnp.sum(d_second * normed2, axis=0)), lax.optimization_barrier(jnp.sum(d_second, axis=0)), lax.optimization_barrier(jnp.sum(d_upper, axis=0)), lax.optimization_barrier(jnp.sum(grad_top, axis=0))])
    return (output, d_input, (g_qkv, g_out, g_up, g_down, g_vec))

def reference(block_input, out_cotangent, seq_lengths, w_qkv, w_out, w_up, w_down, vectors):
    wqkv = w_qkv.reshape(D, 3 * D)
    wo = w_out.reshape(D, D)
    wup = w_up.reshape(D, FF)
    wdn = w_down.reshape(FF, D)
    vec = vectors.astype(jnp.float32)
    inputs = block_input.reshape(N_DP, TOK_DEV, D)
    cotangents = out_cotangent.reshape(N_DP, TOK_DEV, D)

    def step(carry, item):
        block, cotangent, lengths = item
        output, d_input, grads = device_pass(block, cotangent, lengths, wqkv, wo, wup, wdn, vec)
        return (tuple((total + part for total, part in zip(carry, grads))), (output, d_input))
    start = (jnp.zeros((D, 3 * D), jnp.float32), jnp.zeros((D, D), jnp.float32), jnp.zeros((D, FF), jnp.float32), jnp.zeros((FF, D), jnp.float32), jnp.zeros((8 * D + FF,), jnp.float32))
    totals, (outputs, d_inputs) = lax.scan(step, start, (inputs, cotangents, seq_lengths))
    return (outputs.reshape(TOKENS, D), d_inputs.reshape(TOKENS, D), totals[0].reshape(-1), totals[1].reshape(-1), totals[2].reshape(-1), totals[3].reshape(-1), totals[4])
```

```python
import jax
import jax.numpy as jnp
from jax import lax
from jax.sharding import PartitionSpec as P

HEADS = 17
HEAD_DIM = 64


EPS = 1e-05
ROOT_HALF = 0.7071067811865476
INV_ROOT_TAU = 0.3989422804014327


def layer_norm(rows, gain, shift):
    mean = jnp.mean(rows, axis=1, keepdims=True)
    centered = rows - mean
    inverse = lax.rsqrt(jnp.mean(centered * centered, axis=1, keepdims=True) + EPS)
    normed = centered * inverse
    return (normed, inverse, normed * gain + shift)


def norm_back(grad_rows, normed, inverse, gain):
    scaled = grad_rows * gain
    inner = jnp.mean(scaled * normed, axis=1, keepdims=True)
    return inverse * (scaled - jnp.mean(scaled, axis=1, keepdims=True) - normed * inner)


def gelu_exact(value):
    return 0.5 * value * (1.0 + lax.erf(value * ROOT_HALF))


def gelu_slope(value):
    return (
        0.5 * (1.0 + lax.erf(value * ROOT_HALF))
        + value * jnp.exp(-0.5 * value * value) * INV_ROOT_TAU
    )


def causal_mask(lengths, rows):
    ends = jnp.cumsum(lengths)
    position = jnp.arange(rows, dtype=jnp.int32)
    segment = jnp.sum((position[:, None] >= ends[None, :]).astype(jnp.int32), axis=1)
    return (segment[:, None] == segment[None, :]) & (position[None, :] <= position[:, None])


def score_block(query, keys, mask):
    scores = jnp.einsum("qhe,khe->hqk", query, keys, preferred_element_type=jnp.float32)
    return jnp.where(mask[None], scores, -1e30)


def shape_params(flat_parts, width):
    hidden = 4 * width
    return (
        flat_parts[0].reshape(width, 3 * width),
        flat_parts[1].reshape(width, width),
        flat_parts[2].reshape(width, hidden),
        flat_parts[3].reshape(hidden, width),
        flat_parts[4].astype(jnp.float32),
    )


def window_term(left_rows, right_rows, flat_start, flat_count):
    inner_len = left_rows.shape[1]
    columns = right_rows.shape[1]
    row_count = min(inner_len, flat_count // columns + 2)
    row_first = jnp.clip(flat_start // columns, 0, inner_len - row_count)
    product = lax.dot_general(
        left_rows, right_rows, (((0,), (0,)), ((), ())), preferred_element_type=jnp.float32
    ).reshape(-1)
    padded = jnp.concatenate([product, jnp.zeros((flat_count,), jnp.float32)])
    return lax.dynamic_slice_in_dim(padded, flat_start - row_first * columns, flat_count, 0)


def shard_terms(pairs, vector_grad, device_total):
    piece_lens = [
        left_rows.shape[1] * right_rows.shape[1] // device_total for left_rows, right_rows in pairs
    ]
    piece_lens = piece_lens + [vector_grad.shape[0] // device_total]
    shard_len = sum(piece_lens)

    def shard_term(start, count):
        dev_count = count // shard_len
        dev_first = start // shard_len
        pieces = []
        for (left_rows, right_rows), piece_len in zip(pairs, piece_lens):
            window = window_term(
                left_rows, right_rows, dev_first * piece_len, dev_count * piece_len
            )
            pieces.append(window.reshape(dev_count, piece_len))
        vec_len = piece_lens[-1]
        window = vector_grad
        pieces.append(window.reshape(dev_count, vec_len))
        return jnp.concatenate(pieces, axis=1).reshape(-1)

    return (shard_term, shard_len, piece_lens)


def split_shard(summed, piece_lens):
    outputs = []
    offset = 0
    for piece_len in piece_lens:
        outputs.append(summed[offset : offset + piece_len])
        offset = offset + piece_len
    return outputs


def fetch_flat(w_qkv, w_out, w_up, w_down, vectors, width):
    fetched = tuple(
        lax.all_gather(part, "dp", axis=0, tiled=True)
        for part in (w_qkv, w_out, w_up, w_down, vectors)
    )
    return shape_params(fetched, width)


def reduce_flat(pairs, g_vec, device_total):
    all_term, all_len, all_lens = shard_terms(pairs, g_vec, device_total)
    return split_shard(
        lax.psum_scatter(
            all_term(jnp.int32(0), all_len * device_total),
            "dp",
            scatter_dimension=0,
            tiled=True,
        ),
        all_lens,
    )


def fetch_rows(w_qkv, w_out, w_up, w_down, vectors, width, total):
    own = width // total
    count = vectors.shape[0]
    side = jnp.concatenate([w_qkv.reshape(own, 3 * width), w_out.reshape(own, width)], axis=1)
    extra = jnp.pad(vectors, (0, 4 * width - count)).reshape(1, 4 * width)
    side = lax.all_gather(jnp.concatenate([side, extra], axis=0), "dp", axis=0, tiled=False)
    wup = lax.all_gather(w_up.reshape(own, 4 * width), "dp", axis=0, tiled=False)
    wdn = lax.all_gather(w_down.reshape(4 * own, width), "dp", axis=0, tiled=True)
    both = side[:, :own].reshape(width, 4 * width)
    vec = side[:, own, :count].reshape(-1).astype(jnp.float32)
    return both[:, : 3 * width], both[:, 3 * width :], wup.reshape(width, 4 * width), wdn, vec


def product_low(left_rows, right_rows):
    return lax.dot_general(
        left_rows, right_rows, (((0,), (0,)), ((), ())), preferred_element_type=jnp.float32
    ).astype(jnp.bfloat16)


def reduce_rows(pairs, g_vec, total):
    width = pairs[0][0].shape[1]
    own = width // total
    count = g_vec.shape[0] // total
    low = [product_low(left, right) for left, right in pairs]
    down = lax.psum_scatter(low[3], "dp", scatter_dimension=0, tiled=True)
    up = lax.psum_scatter(
        low[2].reshape(total, own, 4 * width), "dp", scatter_dimension=0, tiled=False
    )
    side = jnp.concatenate([low[0], low[1]], axis=1).reshape(total, own, 4 * width)
    extra = jnp.pad(
        g_vec.reshape(total, 1, count).astype(jnp.bfloat16),
        ((0, 0), (0, 0), (0, 4 * width - count)),
    )
    side = lax.psum_scatter(
        jnp.concatenate([side, extra], axis=1), "dp", scatter_dimension=0, tiled=False
    )
    parts = (
        side[:own, : 3 * width],
        side[:own, 3 * width :],
        up,
        down,
        side[own, :count],
    )
    return [part.astype(jnp.float32).reshape(-1) for part in parts]


def body(block_input, out_cotangent, seq_lengths, w_qkv, w_out, w_up, w_down, vectors):
    rows, width = block_input.shape
    hidden = 4 * width
    scale = HEAD_DIM ** (-0.5)
    device_total = lax.axis_size("dp")
    mask = causal_mask(seq_lengths[0], rows)
    by_rows = width % device_total == 0 and vectors.shape[0] <= hidden
    if by_rows:
        wqkv, wo, wup, wdn, vec = fetch_rows(
            w_qkv, w_out, w_up, w_down, vectors, width, device_total
        )
    else:
        wqkv, wo, wup, wdn, vec = fetch_flat(w_qkv, w_out, w_up, w_down, vectors, width)
    inputs = block_input.astype(jnp.float32)
    normed1, inverse1, pre1 = layer_norm(inputs, vec[0:width], vec[width : 2 * width])
    first = pre1.astype(jnp.bfloat16)
    qkv = jnp.dot(first, wqkv, preferred_element_type=jnp.float32)
    query = (
        ((qkv[:, 0:width] + vec[2 * width : 3 * width]) * scale)
        .astype(jnp.bfloat16)
        .reshape(rows, HEADS, HEAD_DIM)
    )
    keys = qkv[:, width : 2 * width].astype(jnp.bfloat16).reshape(rows, HEADS, HEAD_DIM)
    values = (
        (qkv[:, 2 * width : 3 * width] + vec[3 * width : 4 * width])
        .astype(jnp.bfloat16)
        .reshape(rows, HEADS, HEAD_DIM)
    )
    scores = score_block(query, keys, mask)
    peak = jnp.max(scores, axis=2, keepdims=True)
    logsum = peak + jnp.log(jnp.sum(jnp.exp(scores - peak), axis=2, keepdims=True))
    probs_low = jnp.exp(scores - logsum).astype(jnp.bfloat16)
    mixed = jnp.einsum("hqk,khe->qhe", probs_low, values, preferred_element_type=jnp.float32)
    mixed = mixed.astype(jnp.bfloat16).reshape(rows, width)
    resid = (
        inputs + jnp.dot(mixed, wo, preferred_element_type=jnp.float32) + vec[4 * width : 5 * width]
    )
    normed2, inverse2, pre2 = layer_norm(
        resid, vec[5 * width : 6 * width], vec[6 * width : 7 * width]
    )
    second = pre2.astype(jnp.bfloat16)
    upper = (
        jnp.dot(second, wup, preferred_element_type=jnp.float32)
        + vec[7 * width : 7 * width + hidden]
    )
    active = gelu_exact(upper).astype(jnp.bfloat16)
    output = (
        resid + jnp.dot(active, wdn, preferred_element_type=jnp.float32) + vec[7 * width + hidden :]
    )
    block_output = output.astype(jnp.bfloat16)
    back_w = (wqkv, wo, wup, wdn)
    bqkv, bwo, bwup, bwdn = back_w
    grad_top = out_cotangent.astype(jnp.float32)
    d_upper = jnp.dot(out_cotangent, bwdn.T, preferred_element_type=jnp.float32) * gelu_slope(upper)
    d_upper_low = d_upper.astype(jnp.bfloat16)
    d_second = jnp.dot(d_upper_low, bwup.T, preferred_element_type=jnp.float32)
    d_resid = grad_top + norm_back(d_second, normed2, inverse2, vec[5 * width : 6 * width])
    d_resid_low = d_resid.astype(jnp.bfloat16)
    d_mixed = jnp.dot(d_resid_low, bwo.T, preferred_element_type=jnp.float32).astype(jnp.bfloat16)
    d_mixed = d_mixed.reshape(rows, HEADS, HEAD_DIM)
    probs = jnp.exp(score_block(query, keys, mask) - logsum)
    probs_low = probs.astype(jnp.bfloat16)
    d_values = jnp.einsum("hqk,qhe->khe", probs_low, d_mixed, preferred_element_type=jnp.float32)
    d_probs = jnp.einsum("qhe,khe->hqk", d_mixed, values, preferred_element_type=jnp.float32)
    delta = jnp.sum(probs * d_probs, axis=2, keepdims=True)
    d_scores = (probs * (d_probs - delta)).astype(jnp.bfloat16)
    d_query = (
        jnp.einsum("hqk,khe->qhe", d_scores, keys, preferred_element_type=jnp.float32).reshape(
            rows, width
        )
        * scale
    )
    d_keys = jnp.einsum(
        "hqk,qhe->khe", d_scores, query, preferred_element_type=jnp.float32
    ).reshape(rows, width)
    d_values = d_values.reshape(rows, width)
    d_qkv = jnp.concatenate([d_query, d_keys, d_values], axis=1).astype(jnp.bfloat16)
    d_first = jnp.dot(d_qkv, bqkv.T, preferred_element_type=jnp.float32)
    input_grad = d_resid + norm_back(d_first, normed1, inverse1, vec[0:width])
    g_vec = jnp.concatenate(
        [
            jnp.sum(d_first * normed1, axis=0),
            jnp.sum(d_first, axis=0),
            jnp.sum(d_query, axis=0),
            jnp.sum(d_values, axis=0),
            jnp.sum(d_resid, axis=0),
            jnp.sum(d_second * normed2, axis=0),
            jnp.sum(d_second, axis=0),
            jnp.sum(d_upper, axis=0),
            jnp.sum(grad_top, axis=0),
        ]
    )
    pairs = [(first, d_qkv), (mixed, d_resid_low), (second, d_upper_low), (active, out_cotangent)]
    reducer = reduce_rows if by_rows else reduce_flat
    grad_qkv, grad_out, grad_up, grad_down, grad_vectors = reducer(pairs, g_vec, device_total)
    return (block_output, input_grad, grad_qkv, grad_out, grad_up, grad_down, grad_vectors)


def solution(mesh):
    in_specs = (
        P("dp", None),
        P("dp", None),
        P("dp", None),
        P("dp"),
        P("dp"),
        P("dp"),
        P("dp"),
        P("dp"),
    )
    out_specs = (P("dp", None), P("dp", None), P("dp"), P("dp"), P("dp"), P("dp"), P("dp"))
    return jax.shard_map(body, mesh=mesh, in_specs=in_specs, out_specs=out_specs, check_vma=False)
```
